512 devices in a mesh: tm: 4 (over z_hi), space: 128 (over z_lo, x, y, core).
Axes of the slice: x: 4, y: 8, z: 8 (z_hi: 4, z_lo: 2; z = z_hi * 2 + z_lo), core: 2. Of those that a mesh axis runs over, the one named last changes fastest.
Arguments:
- frames: bfloat16 [4, 73, 1024, 1024], P('tm', None, None, 'space'), may hold values from -6 to 6
- regrid_mats: bfloat16 [16, 64, 144], replicated, may hold values from -0.75 to 0.75
- pair_source: int32 [16384], P('space'), may hold values from 0 to 127
- pair_matrix: int32 [16384], P('space'), may hold values from 0 to 15
- pair_device: int32 [16384, 1], P('space'), may hold values from 0 to 127; in each aligned block of 128 rows (0 to 127, 128 to 255, ...) at most 2 rows name the same one
- pair_local: int32 [16384], P('space'), may hold values from 0 to 11
- w_first: bfloat16 [3, 3, 73, 256], replicated, may hold values from -0.25 to 0.25
- b_first: float32 [256], replicated, may hold values from -3 to 3
- w_second: bfloat16 [3, 3, 256, 256], replicated, may hold values from -0.125 to 0.125
- b_second: float32 [256], replicated, may hold values from -3 to 3
Outputs:
- features: bfloat16 [4, 1536, 64, 256], P('tm', 'space')
The draws below stay inside these ranges and needn't reach their ends.
Inputs may be any that keep to these rules, and one draw needn't show every extreme that they name: `pair_device`: among the 128 rows of one device no device number appears more than 2 times, and in every draw some device's rows name one device exactly 2 times.
All inputs are finite; a program needn't handle non-finite values.
Results may differ from the reference program's by a relative error of at most 0.0064.
Values may be sent and summed in bfloat16 or wider, within the bound.
No kernel may reach another device: no remote copies, remote signals or barrier semaphores. Data moves between devices by JAX's collectives and lax.ppermute only.
A program may use at most 64 MiB of HBM per device.

```python
import math
import jax
import jax.numpy as jnp
import numpy as np
from jax import lax

VARS = 73
CH = 256
SIDE = 8
LON = 1024
SB = 64
NMAT = 16
PAIRS_DEV = 128
BLK_DEV = 12
TIMES = 4
LAT = 1024
SRC_DEV = 128
BLOCKS = 1536
PAD_SIDE = 12
PAD_CELLS = 144
CAP = 2
N_SPACE = 128


def place_ends(drawn, own_key, least, largest):
    index_at = [jax.random.randint(jax.random.fold_in(own_key, axis), (), 0, length) for axis, length in enumerate(drawn.shape)]
    main_axis = drawn.shape.index(max(drawn.shape))
    neighbour = index_at[:main_axis] + [(index_at[main_axis] + 1) % drawn.shape[main_axis]] + index_at[main_axis + 1:]
    return drawn.at[tuple(index_at)].set(least).at[tuple(neighbour)].set(largest)


def levels(key, extent, cuts, least, top_value):
    def one(position, blocks):
        heights = jax.random.uniform(jax.random.fold_in(jax.random.fold_in(key, 6), position), (blocks,), jnp.float32, least / len(cuts), top_value / len(cuts))
        return jnp.repeat(jnp.exp(heights), extent[position] // blocks).reshape((-1,) + (1,) * (len(extent) - position - 1))

    factor_of = one(*cuts[0])
    for cut in cuts[1:]:
        factor_of = factor_of * one(*cut)
    return factor_of


def shared_out(key, own, number, rows, number_of, top, reach, skew):
    order = jax.random.permutation(key, number_of)
    crowded, usual = portions_of(number_of, rows * top, reach, skew, True), portions_of(number_of, rows * top, reach, skew, False)
    places = jnp.arange(number_of)

    def named(tallies, rotation):
        used = int((tallies > 0).sum())
        fixed = max(1, used // 4)
        shifted = fixed + (places - fixed + rotation * (used - fixed)) % max(1, number_of - fixed)
        return jnp.zeros((number_of,), jnp.int32).at[order[jnp.where(places < fixed, places, shifted)]].set(jnp.asarray(tallies, jnp.int32))

    tallies = jnp.where(number % 4 == 0, named(crowded, number // 4), named(usual, number - number // 4 - 1))
    mixed = jax.random.permutation(jax.random.fold_in(own, 3), number_of)
    giver, receiver = mixed[0:number_of // 2 * 2:2], mixed[1:number_of // 2 * 2:2]
    margin = jnp.minimum(tallies[giver] - 1, reach - tallies[receiver]) // 2
    margin = jnp.where((giver == order[0]) | (receiver == order[0]) | (tallies[receiver] == 0), 0, jnp.maximum(margin, 0))
    shifted = jax.random.randint(jax.random.fold_in(own, 4), (number_of // 2,), 0, 1 << 20) % (margin + 1)
    tallies = tallies.at[giver].add(-shifted).at[receiver].add(shifted)
    labels = jnp.searchsorted(jnp.cumsum(tallies), jnp.arange(rows * top), side="right").astype(jnp.int32)
    table = labels.reshape(top, rows).T
    table = table[jax.random.permutation(jax.random.fold_in(own, 1), rows)]
    rotation = jax.random.randint(jax.random.fold_in(own, 2), (rows, 1), 0, top)
    return jnp.take_along_axis(table, (jnp.arange(top)[None, :] + rotation) % top, axis=1)


def portions_of(amount, total, reach, lean, full):
    portions = [(1 << 20) // math.isqrt(standing ** lean) + 1 for standing in range(1, amount + 1)]
    largest = reach if full else min(reach, max(-(-total // amount), total * portions[0] // sum(portions)))
    least = 1 if total - largest >= amount - 1 else 0
    holding, spare = [largest] + [least] * (amount - 1), total - largest - least * (amount - 1)
    while spare > 0:
        movable = [i for i in range(1, amount) if holding[i] < largest] or [i for i in range(1, amount) if holding[i] < reach]
        whole, left = sum([portions[i] for i in movable]), spare
        for i in movable:
            more = min(reach - holding[i], max(1, left * portions[i] // whole), spare)
            holding[i] = holding[i] + more
            spare = spare - more
    return np.array(holding)


def scatter_about(rng, dims, width, most, pieces=(), held_as=jnp.bfloat16):
    factor_of = levels(rng, dims, pieces, -0.22, 0.18) if pieces else 1.0
    result = jax.random.normal(rng, dims, jnp.float32) * width * factor_of
    return jnp.minimum(jnp.maximum(result, -most), most).astype(held_as)


def setup_inputs(seed: int = 0) -> dict:
    keys = jax.random.split(jax.random.key(seed), 11)
    frames = scatter_about(keys[0], (TIMES, VARS, LAT, LON), 1.0, 6.0, ((0, 4), (3, 128)))
    regrid_mats = scatter_about(keys[1], (NMAT, SB, PAD_CELLS), SB ** -0.5, 0.75)
    pair_source = place_ends(jax.random.randint(keys[2], (N_SPACE * PAIRS_DEV,), 0, SRC_DEV), jax.random.fold_in(keys[2], 1), 0, SRC_DEV - 1).astype(jnp.int32)
    pair_matrix = place_ends(jax.random.randint(keys[3], (N_SPACE * PAIRS_DEV,), 0, NMAT), jax.random.fold_in(keys[3], 1), 0, NMAT - 1).astype(jnp.int32)
    pair_device_keys = jax.random.split(jax.random.fold_in(keys[4], 1), (N_SPACE * PAIRS_DEV) // PAIRS_DEV)
    pair_device_turns = jax.random.permutation(jax.random.fold_in(keys[4], 3), (N_SPACE * PAIRS_DEV) // PAIRS_DEV)
    pair_device = jax.vmap(lambda own, number: shared_out(jax.random.fold_in(keys[4], 2), own, number, PAIRS_DEV, N_SPACE, 1, CAP, 2))(pair_device_keys, pair_device_turns).reshape((N_SPACE * PAIRS_DEV, 1))
    pair_local = place_ends(jax.random.randint(keys[5], (N_SPACE * PAIRS_DEV,), 0, BLK_DEV), jax.random.fold_in(keys[5], 1), 0, BLK_DEV - 1).astype(jnp.int32)
    w_first = scatter_about(keys[6], (3, 3, VARS, CH), (9 * VARS) ** -0.5, 0.25)
    b_first = scatter_about(keys[7], (CH,), 0.5, 3.0, (), jnp.float32)
    w_second = scatter_about(keys[8], (3, 3, CH, CH), (9 * CH) ** -0.5, 0.125)
    b_second = scatter_about(keys[9], (CH,), 0.5, 3.0, (), jnp.float32)
    return {"frames": frames, "regrid_mats": regrid_mats, "pair_source": pair_source, "pair_matrix": pair_matrix, "pair_device": pair_device, "pair_local": pair_local, "w_first": w_first, "b_first": b_first, "w_second": w_second, "b_second": b_second}


def conv_valid(inputs, weights, layout):
    return lax.conv_general_dilated(inputs, weights, (1, 1), "VALID", dimension_numbers=layout, precision=lax.Precision.HIGHEST, preferred_element_type=jnp.float32)


def encode(group_field, w_first, b_first, w_second, b_second):
    block_count = group_field.shape[0]
    images = group_field.reshape(block_count * TIMES, VARS, PAD_SIDE, PAD_SIDE).astype(jnp.float32)
    first_out = conv_valid(images, w_first.astype(jnp.float32), ("NCHW", "HWIO", "NHWC")) + b_first
    hidden = jax.nn.gelu(first_out, approximate=True).astype(jnp.bfloat16)
    second = conv_valid(hidden.astype(jnp.float32), w_second.astype(jnp.float32), ("NHWC", "HWIO", "NHWC")) + b_second
    return second.astype(jnp.bfloat16).reshape(block_count, TIMES, SIDE * SIDE, CH)


def reference(frames, regrid_mats, pair_source, pair_matrix, pair_device, pair_local, w_first, b_first, w_second, b_second):
    source = frames.reshape(TIMES, VARS, N_SPACE * SRC_DEV, SB)
    source_rows = pair_source.reshape(N_SPACE, PAIRS_DEV)
    matrix_rows = pair_matrix.reshape(N_SPACE, PAIRS_DEV)
    target_rows = (pair_device[:, 0] * BLK_DEV + pair_local).astype(jnp.int32).reshape(N_SPACE, PAIRS_DEV)

    def add_sender(padded_field, inputs):
        sender, source_ids, matrix_ids, block_ids = inputs
        picked = jnp.take(source, (sender * SRC_DEV + source_ids).astype(jnp.int32), axis=2).astype(jnp.float32)
        matrices = jnp.take(regrid_mats, matrix_ids, axis=0).astype(jnp.float32)
        partial_value = jnp.einsum("tvps,psc->ptvc", picked, matrices, precision=lax.Precision.HIGHEST).astype(jnp.bfloat16)
        return padded_field.at[block_ids].add(partial_value.astype(jnp.float32)), None

    padded_field = jnp.zeros((BLOCKS, TIMES, VARS, PAD_CELLS), jnp.float32)
    senders = jnp.arange(N_SPACE, dtype=jnp.int32)
    padded_field, unused = lax.scan(add_sender, padded_field, (senders, source_rows, matrix_rows, target_rows))
    grouped = padded_field.astype(jnp.bfloat16).reshape(N_SPACE, BLK_DEV, TIMES, VARS, PAD_SIDE, PAD_SIDE)
    encoded = lax.map(lambda group_field: encode(group_field, w_first, b_first, w_second, b_second), grouped)
    return jnp.transpose(encoded.reshape(BLOCKS, TIMES, SIDE * SIDE, CH), (1, 0, 2, 3))
```

```python
import jax
import jax.numpy as jnp
from jax import lax
from jax.experimental import pallas as pl
from jax.experimental.pallas import tpu as pltpu
from jax.sharding import PartitionSpec as P

SIDE = 8
BLK_DEV = 12
PAD_SIDE = 12
VPAD = 80
LANES = 128
META_BLOCK = 73
META_MATRIX = 74
INTERPRET = False


def conv_valid(inputs, weights, layout):
    return lax.conv_general_dilated(
        inputs,
        weights,
        (1, 1),
        "VALID",
        dimension_numbers=layout,
        preferred_element_type=jnp.float32,
    )


def pack_kernel(x_ref, o_ref, perm_ref):
    @pl.when(pl.program_id(0) == 0)
    def _():
        row = lax.broadcasted_iota(jnp.int32, perm_ref.shape, 0)
        col = lax.broadcasted_iota(jnp.int32, perm_ref.shape, 1)
        wanted = (row & 7) * VPAD + (row >> 3)
        perm_ref[...] = jnp.where(col == wanted, 1.0, 0.0).astype(jnp.bfloat16)

    o_ref[...] = lax.dot_general(
        x_ref[...], perm_ref[...], (((0,), (0,)), ((), ())), preferred_element_type=jnp.float32
    ).astype(jnp.bfloat16)


def pack_frames(frames):
    _, variables, lats, lons = frames.shape
    rows = frames.transpose(0, 1, 3, 2).reshape(variables * lons, lats)
    width = lons * VPAD
    step = 256
    return pl.pallas_call(
        pack_kernel,
        grid=(lats // step,),
        in_specs=[pl.BlockSpec((variables * lons, step), lambda i: (0, i))],
        out_specs=pl.BlockSpec((step, width), lambda i: (i, 0)),
        out_shape=jax.ShapeDtypeStruct((lats, width), jnp.bfloat16),
        scratch_shapes=[pltpu.VMEM((variables * lons, width), jnp.bfloat16)],
        interpret=INTERPRET,
    )(rows)


def select_kernel(pick_ref, meta_ref, x_ref, o_ref):
    out = lax.dot_general(
        pick_ref[...], x_ref[...], (((1,), (0,)), ((), ())), preferred_element_type=jnp.float32
    )
    o_ref[:, LANES:] = out[:, LANES:].astype(jnp.bfloat16)
    o_ref[:, :LANES] = (out[:, :LANES] + meta_ref[...].astype(jnp.float32)).astype(jnp.bfloat16)


def select_rows(pick, meta, rows):
    count, depth = pick.shape
    width = rows.shape[1]
    step = 512
    return pl.pallas_call(
        select_kernel,
        grid=(count // step,),
        in_specs=[
            pl.BlockSpec((step, depth), lambda i: (i, 0)),
            pl.BlockSpec((step, LANES), lambda i: (i, 0)),
            pl.BlockSpec((depth, width), lambda i: (0, 0)),
        ],
        out_specs=pl.BlockSpec((step, width), lambda i: (i, 0)),
        out_shape=jax.ShapeDtypeStruct((count, width), jnp.bfloat16),
        interpret=INTERPRET,
    )(pick, meta, rows)


def regrid_kernel(r_ref, mats_ref, o_ref):
    rows = r_ref[...]
    count = rows.shape[0]
    kind = lax.broadcasted_iota(jnp.int32, (LANES, LANES), 0)
    weight = jnp.where(kind == META_BLOCK, 128.0, jnp.where(kind == META_MATRIX, 8.0, 0.0))
    code = jnp.dot(
        rows[:, :LANES], weight.astype(jnp.bfloat16), preferred_element_type=jnp.float32
    )
    lane = lax.broadcasted_iota(jnp.int32, (count, LANES), 1)
    step = lax.broadcasted_iota(jnp.int32, (count, LANES), 0) & 7
    code = code - (lane - step).astype(jnp.float32)
    turned = rows.T
    mats = mats_ref[...]
    for block in range(BLK_DEV):
        mine = jnp.where(code == (block + 1) * 128.0, 1.0, 0.0).astype(jnp.bfloat16)
        gathered = jnp.dot(turned, mine, preferred_element_type=jnp.float32).astype(jnp.bfloat16)
        stacked = jnp.concatenate(
            [gathered[w * VPAD : (w + 1) * VPAD] for w in range(8)], axis=1
        )
        field = lax.dot_general(
            mats, stacked, (((1,), (1,)), ((), ())), preferred_element_type=jnp.float32
        )
        o_ref[block] = field.astype(jnp.bfloat16)


def regrid(rows, mats):
    cells = mats.shape[0]
    return pl.pallas_call(
        regrid_kernel,
        out_shape=jax.ShapeDtypeStruct((BLK_DEV, cells, VPAD), jnp.bfloat16),
        interpret=INTERPRET,
    )(rows, mats)


def per_device(
    frames,
    regrid_mats,
    pair_source,
    pair_matrix,
    pair_device,
    pair_local,
    w_first,
    b_first,
    w_second,
    b_second,
):
    devices = lax.axis_size("space")
    variables = frames.shape[1]
    count = pair_source.shape[0]
    packed = pack_frames(frames)
    width = packed.shape[1]
    lats = packed.shape[0]
    band = lats // devices
    strips = lax.all_to_all(
        packed.reshape(devices, band, width), "space", split_axis=0, concat_axis=0, tiled=True
    ).reshape(lats, width)

    target = pair_device[:, 0]
    order = jnp.arange(count, dtype=jnp.int32)
    earlier = (target[:, None] == target[None, :]) & (order[:, None] < order[None, :])
    rank = jnp.sum(earlier.astype(jnp.int32), axis=0)
    place = target * 2 + rank
    columns = devices // 8
    first_row = (pair_source % columns) * 64 + pair_source // columns
    row = jnp.arange(devices * 16, dtype=jnp.int32)
    hit = (place[None, :] == (row >> 3)[:, None]).astype(jnp.int32)
    shift = 16384
    wanted = jnp.sum(hit * (first_row + shift)[None, :], axis=1) + (row & 7) * 8
    block = jnp.sum(hit * (pair_local + 1)[None, :], axis=1)
    matrix = jnp.sum(hit * pair_matrix[None, :], axis=1)
    pick = (wanted[:, None] == (jnp.arange(lats, dtype=jnp.int32) + shift)[None, :]).astype(
        jnp.bfloat16
    )
    lane = jnp.arange(LANES, dtype=jnp.int32)[None, :]
    meta = jnp.where(
        lane == META_BLOCK, block[:, None], jnp.where(lane == META_MATRIX, matrix[:, None], 0)
    ).astype(jnp.bfloat16)

    outgoing = select_rows(pick, meta, strips)
    received = lax.all_to_all(
        outgoing.reshape(devices, 16, width), "space", split_axis=0, concat_axis=0, tiled=True
    ).reshape(devices * 16, width)

    kinds, _, cells = regrid_mats.shape
    mats = regrid_mats.reshape(kinds, 8, 8, cells).transpose(3, 2, 0, 1).reshape(cells, kinds * 64)
    field = regrid(received, mats)
    padded_field = field.reshape(BLK_DEV, PAD_SIDE, PAD_SIDE, VPAD)[..., :variables]
    first_out = conv_valid(padded_field, w_first, ("NHWC", "HWIO", "NHWC")) + b_first
    hidden = jax.nn.gelu(first_out, approximate=True).astype(jnp.bfloat16)
    second = conv_valid(hidden, w_second, ("NHWC", "HWIO", "NHWC")) + b_second
    return second.astype(jnp.bfloat16).reshape(1, BLK_DEV, SIDE * SIDE, -1)


def solution(mesh):
    in_specs = (
        P("tm", None, None, "space"),
        P(),
        P("space"),
        P("space"),
        P("space", None),
        P("space"),
        P(),
        P(),
        P(),
        P(),
    )
    out_specs = P("tm", "space", None, None)
    return jax.shard_map(
        per_device, mesh=mesh, in_specs=in_specs, out_specs=out_specs, check_vma=False
    )
```

```python
import jax
import jax.numpy as jnp
from jax import lax
from jax.experimental import pallas as pl
from jax.experimental.pallas import tpu as pltpu
from jax.sharding import PartitionSpec as P

SIDE = 8
BLK_DEV = 12
PAD_SIDE = 12
VPAD = 80
LANES = 128
META_BLOCK = 73
META_MATRIX = 74
INTERPRET = False


def conv_valid(inputs, weights, layout):
    return lax.conv_general_dilated(
        inputs,
        weights,
        (1, 1),
        "VALID",
        dimension_numbers=layout,
        preferred_element_type=jnp.float32,
    )


def pack_kernel(x_ref, o_ref, perm_ref):
    @pl.when(pl.program_id(0) == 0)
    def _():
        row = lax.broadcasted_iota(jnp.int32, perm_ref.shape, 0)
        col = lax.broadcasted_iota(jnp.int32, perm_ref.shape, 1)
        wanted = (row & 7) * VPAD + (row >> 3)
        perm_ref[...] = jnp.where(col == wanted, 1.0, 0.0).astype(jnp.bfloat16)

    o_ref[...] = lax.dot_general(
        x_ref[...], perm_ref[...], (((0,), (0,)), ((), ())), preferred_element_type=jnp.float32
    ).astype(jnp.bfloat16)


def pack_frames(rows):
    depth, lats = rows.shape
    width = 8 * VPAD
    step = 256
    return pl.pallas_call(
        pack_kernel,
        grid=(lats // step,),
        in_specs=[pl.BlockSpec((depth, step), lambda i: (0, i))],
        out_specs=pl.BlockSpec((step, width), lambda i: (i, 0)),
        out_shape=jax.ShapeDtypeStruct((lats, width), jnp.bfloat16),
        scratch_shapes=[pltpu.VMEM((depth, width), jnp.bfloat16)],
        interpret=INTERPRET,
    )(rows)


def select_kernel(pick_ref, meta_ref, x_ref, o_ref):
    width = x_ref.shape[-1]
    for half in range(2):
        x = x_ref[:, half].reshape(pick_ref.shape[1], width)
        out = jnp.dot(pick_ref[...], x, preferred_element_type=jnp.float32)
        if half == 0:
            meta = meta_ref[...].astype(jnp.float32)
            o_ref[:, :LANES] = (out[:, :LANES] + meta).astype(jnp.bfloat16)
            o_ref[:, LANES:width] = out[:, LANES:].astype(jnp.bfloat16)
        else:
            o_ref[:, width:] = out.astype(jnp.bfloat16)


def select_rows(pick, meta, strips):
    count, depth = pick.shape
    width = strips.shape[-1]
    strips = strips.reshape(-1, 2, 32, width)
    step = 256
    return pl.pallas_call(
        select_kernel,
        grid=(count // step,),
        in_specs=[
            pl.BlockSpec((step, depth), lambda i: (i, 0)),
            pl.BlockSpec((step, LANES), lambda i: (i, 0)),
            pl.BlockSpec(strips.shape, lambda i: (0, 0, 0, 0)),
        ],
        out_specs=pl.BlockSpec((step, 2 * width), lambda i: (i, 0)),
        out_shape=jax.ShapeDtypeStruct((count, 2 * width), jnp.bfloat16),
        interpret=INTERPRET,
    )(pick, meta, strips)


def regrid_kernel(r_ref, even_ref, odd_ref, o_ref, sum_ref, code_ref):
    half = pl.program_id(0)
    count = r_ref.shape[0]

    @pl.when(half == 0)
    def _():
        kind = lax.broadcasted_iota(jnp.int32, (LANES, 2 * LANES), 0)
        weight = jnp.where(kind == META_BLOCK, 64.0, jnp.where(kind == META_MATRIX, 4.0, 0.0))
        step = lax.broadcasted_iota(jnp.int32, code_ref.shape, 0) & 3
        code_ref[...] = step.astype(jnp.float32) + jnp.dot(
            r_ref[:, :LANES], weight.astype(jnp.bfloat16), preferred_element_type=jnp.float32
        )

    lane = lax.broadcasted_iota(jnp.int32, (1, 2 * LANES), 1)
    code = code_ref[...] - (lane ^ (64 * half)).astype(jnp.float32)
    turned = r_ref[...].T
    for four in range(BLK_DEV // 4):
        mine = jnp.where(code == (4 * four + 1) * 64.0, 1.0, 0.0).astype(jnp.bfloat16)
        got = jnp.dot(turned, mine, preferred_element_type=jnp.float32)
        sum_ref[half, :, four * 256 : (four + 1) * 256] = got.astype(jnp.bfloat16)

    @pl.when(half == 1)
    def _():
        low = lax.broadcasted_iota(jnp.int32, (VPAD, LANES), 1) < 64
        for pair in range(BLK_DEV // 2):
            lanes = slice(pair * LANES, (pair + 1) * LANES)
            one = [sum_ref[0, w * VPAD : (w + 1) * VPAD, lanes] for w in range(8)]
            two = [sum_ref[1, w * VPAD : (w + 1) * VPAD, lanes] for w in range(8)]
            for odd, mats_ref in enumerate((even_ref, odd_ref)):
                left, right = (two, one) if odd else (one, two)
                stacked = jnp.concatenate(
                    [jnp.where(low, left[w], right[w]) for w in range(8)], axis=1
                )
                field = lax.dot_general(
                    mats_ref[...],
                    stacked,
                    (((1,), (1,)), ((), ())),
                    preferred_element_type=jnp.float32,
                )
                o_ref[2 * pair + odd] = field.astype(jnp.bfloat16)


def regrid(rows, even, odd):
    cells = even.shape[0]
    count, width = rows.shape
    return pl.pallas_call(
        regrid_kernel,
        grid=(2,),
        in_specs=[
            pl.BlockSpec((count, width // 2), lambda i: (0, i)),
            pl.BlockSpec(even.shape, lambda i: (0, 0)),
            pl.BlockSpec(odd.shape, lambda i: (0, 0)),
        ],
        out_specs=pl.BlockSpec((BLK_DEV, cells, VPAD), lambda i: (0, 0, 0)),
        out_shape=jax.ShapeDtypeStruct((BLK_DEV, cells, VPAD), jnp.bfloat16),
        scratch_shapes=[
            pltpu.VMEM((2, width // 2, BLK_DEV * 64), jnp.bfloat16),
            pltpu.VMEM((count, 2 * LANES), jnp.float32),
        ],
        interpret=INTERPRET,
    )(rows, even, odd)


def per_device(
    frames,
    regrid_mats,
    pair_source,
    pair_matrix,
    pair_device,
    pair_local,
    w_first,
    b_first,
    w_second,
    b_second,
):
    devices = lax.axis_size("space")
    _, variables, lats, lons = frames.shape
    count = pair_source.shape[0]
    band = lats // devices
    turned = frames.transpose(0, 1, 3, 2).reshape(variables * lons, lats)

    def spread(rows):
        return lax.all_to_all(
            rows.reshape(devices, -1, rows.shape[1]), "space", split_axis=0, concat_axis=0, tiled=True
        ).reshape(rows.shape)

    strips = spread(pack_frames(turned))

    target = pair_device[:, 0]
    order = jnp.arange(count, dtype=jnp.int32)
    earlier = (target[:, None] == target[None, :]) & (order[:, None] < order[None, :])
    rank = jnp.sum(earlier.astype(jnp.int32), axis=0)
    place = target * 2 + rank
    columns = devices // 8
    first_row = (pair_source % columns) * 32 + pair_source // columns
    row = jnp.arange(devices * 8, dtype=jnp.int32)
    hit = (place[None, :] == (row >> 2)[:, None]).astype(jnp.int32)
    shift = 16384
    wanted = jnp.sum(hit * (first_row + shift)[None, :], axis=1) + (row & 3) * band
    block = jnp.sum(hit * (pair_local + 1)[None, :], axis=1)
    matrix = jnp.sum(hit * pair_matrix[None, :], axis=1)
    pick = (wanted[:, None] == (jnp.arange(lats // 2, dtype=jnp.int32) + shift)[None, :]).astype(
        jnp.bfloat16
    )
    lane = jnp.arange(LANES, dtype=jnp.int32)[None, :]
    meta = jnp.where(
        lane == META_BLOCK, block[:, None], jnp.where(lane == META_MATRIX, matrix[:, None], 0)
    ).astype(jnp.bfloat16)

    received = spread(select_rows(pick, meta, strips))

    kinds, _, cells = regrid_mats.shape
    split = regrid_mats.reshape(kinds, 2, 4, 8, cells).transpose(4, 3, 1, 0, 2)
    even = split.reshape(cells, -1)
    odd = split[:, :, ::-1].reshape(cells, -1)
    field = regrid(received, even, odd)
    padded_field = field.reshape(BLK_DEV, PAD_SIDE, PAD_SIDE, VPAD)[..., :variables]
    first_out = conv_valid(padded_field, w_first, ("NHWC", "HWIO", "NHWC")) + b_first
    hidden = jax.nn.gelu(first_out, approximate=True).astype(jnp.bfloat16)
    second = conv_valid(hidden, w_second, ("NHWC", "HWIO", "NHWC")) + b_second
    return second.astype(jnp.bfloat16).reshape(1, BLK_DEV, SIDE * SIDE, -1)


def solution(mesh):
    in_specs = (
        P("tm", None, None, "space"),
        P(),
        P("space"),
        P("space"),
        P("space", None),
        P("space"),
        P(),
        P(),
        P(),
        P(),
    )
    out_specs = P("tm", "space", None, None)
    return jax.shard_map(
        per_device, mesh=mesh, in_specs=in_specs, out_specs=out_specs, check_vma=False
    )
```

```python
import jax
import jax.numpy as jnp
from jax import lax
from jax.experimental import pallas as pl
from jax.experimental.pallas import tpu as pltpu
from jax.sharding import PartitionSpec as P

SIDE = 8
BLK_DEV = 12
PAD_SIDE = 12
VPAD = 80
LANES = 128
META_BLOCK = 72
META_MATRIX = 73
INTERPRET = False


def resident(array):
    return array if INTERPRET else pltpu.with_memory_space_constraint(array, pltpu.VMEM)


def resident_output(shape):
    struct = jax.ShapeDtypeStruct(shape, jnp.bfloat16)
    return struct if INTERPRET else pltpu.VMEM(shape, jnp.bfloat16)


IN_VMEM = pl.BlockSpec(memory_space=pltpu.VMEM)


def conv_valid(inputs, weights, layout):
    return lax.conv_general_dilated(
        inputs,
        weights,
        (1, 1),
        "VALID",
        dimension_numbers=layout,
        preferred_element_type=jnp.float32,
    )


def pack_kernel(x_ref, o_ref):
    depth = x_ref.shape[0]
    count, width = o_ref.shape
    o_ref[:, :depth] = x_ref[...].T
    o_ref[:, depth:] = jnp.zeros((count, width - depth), jnp.bfloat16)


def pack_frames(rows):
    depth, lats = rows.shape
    width = 8 * VPAD
    step = 256
    return pl.pallas_call(
        pack_kernel,
        grid=(lats // step,),
        in_specs=[pl.BlockSpec((depth, step), lambda i: (0, i))],
        out_specs=pl.BlockSpec((step, width), lambda i: (i, 0)),
        out_shape=jax.ShapeDtypeStruct((lats, width), jnp.bfloat16),
        interpret=INTERPRET,
    )(rows)


def select_kernel(pick_ref, meta_ref, x_ref, o_ref):
    depth = pick_ref.shape[1]
    width = x_ref.shape[-1]
    tile = width - LANES
    x = jnp.concatenate([x_ref[:, half].reshape(depth, width) for half in range(2)], axis=1)
    out = jnp.dot(pick_ref[...], x, preferred_element_type=jnp.float32)
    o_ref[:, :tile] = out[:, :tile].astype(jnp.bfloat16)
    meta = meta_ref[...].astype(jnp.float32)
    o_ref[:, tile:width] = (out[:, tile:width] + meta).astype(jnp.bfloat16)
    o_ref[:, width:] = out[:, width:].astype(jnp.bfloat16)


def select_rows(pick, meta, strips):
    count = pick.shape[0]
    width = strips.shape[-1]
    strips = strips.reshape(-1, 2, 32, width)
    step = 256
    return pl.pallas_call(
        select_kernel,
        grid=(count // step,),
        in_specs=[
            pl.BlockSpec((step, pick.shape[1]), lambda i: (i, 0)),
            pl.BlockSpec((step, LANES), lambda i: (i, 0)),
            IN_VMEM,
        ],
        out_specs=pl.BlockSpec((step, 2 * width), lambda i: (i, 0)),
        out_shape=jax.ShapeDtypeStruct((count, 2 * width), jnp.bfloat16),
        interpret=INTERPRET,
    )(pick, meta, resident(strips))


def regrid_kernel(r_ref, even_ref, odd_ref, o_ref, sum_ref, code_ref, turn_ref):
    half = pl.program_id(0)
    width = r_ref.shape[1]

    @pl.when(half == 0)
    def _():
        kind = lax.broadcasted_iota(jnp.int32, (LANES, 2 * LANES), 0)
        weight = jnp.where(kind == META_BLOCK, 64.0, jnp.where(kind == META_MATRIX, 4.0, 0.0))
        step = lax.broadcasted_iota(jnp.int32, code_ref.shape, 0) & 3
        code_ref[...] = step.astype(jnp.float32) + jnp.dot(
            r_ref[:, -LANES:], weight.astype(jnp.bfloat16), preferred_element_type=jnp.float32
        )

    lane = lax.broadcasted_iota(jnp.int32, (1, 2 * LANES), 1)
    code = code_ref[...] - (lane ^ (64 * half)).astype(jnp.float32)
    turned = r_ref[...].T
    for four in range(BLK_DEV // 4):
        mine = jnp.where(code == (4 * four + 1) * 64.0, 1.0, 0.0).astype(jnp.bfloat16)
        got = jnp.dot(turned, mine, preferred_element_type=jnp.float32)
        for side in range(2):
            first = (half * (BLK_DEV // 2) + 2 * four + side) * width
            lanes = slice(side * LANES, (side + 1) * LANES)
            sum_ref[pl.ds(pl.multiple_of(first, width), width), :] = got[:, lanes]

    @pl.when(half == 1)
    def _():
        low = lax.broadcasted_iota(jnp.int32, (VPAD, LANES), 1) < 64
        for pair in range(BLK_DEV // 2):
            one, two = (
                [
                    sum_ref[pl.ds((side * (BLK_DEV // 2) + pair) * width + w, VPAD, stride=8), :]
                    for w in range(8)
                ]
                for side in range(2)
            )
            for odd, mats_ref in enumerate((even_ref, odd_ref)):
                left, right = (two, one) if odd else (one, two)
                stacked = jnp.concatenate(
                    [jnp.where(low, left[w], right[w]).astype(jnp.bfloat16) for w in range(8)],
                    axis=1,
                )
                field = lax.dot_general(
                    mats_ref[...],
                    stacked,
                    (((1,), (1,)), ((), ())),
                    preferred_element_type=jnp.float32,
                )
                turn_ref[pl.ds(2 * pair + odd, field.shape[0], stride=16), :VPAD] = field
        cells = o_ref.shape[0]
        o_ref[...] = (
            turn_ref[...].reshape(cells, 16, LANES)[:, :BLK_DEV, :VPAD].astype(jnp.bfloat16)
        )


def regrid(rows, even, odd):
    cells = even.shape[0]
    count, width = rows.shape
    return pl.pallas_call(
        regrid_kernel,
        grid=(2,),
        in_specs=[
            pl.BlockSpec((count, width // 2), lambda i: (0, i)),
            IN_VMEM,
            IN_VMEM,
        ],
        out_specs=IN_VMEM,
        out_shape=resident_output((cells, BLK_DEV, VPAD)),
        scratch_shapes=[
            pltpu.VMEM((BLK_DEV // 2 * width, LANES), jnp.float32),
            pltpu.VMEM((count, 2 * LANES), jnp.float32),
            pltpu.VMEM((16 * cells, LANES), jnp.float32),
        ],
        interpret=INTERPRET,
    )(rows, resident(even), resident(odd))


def per_device(
    frames,
    regrid_mats,
    pair_source,
    pair_matrix,
    pair_device,
    pair_local,
    w_first,
    b_first,
    w_second,
    b_second,
):
    devices = lax.axis_size("space")
    _, variables, lats, lons = frames.shape
    count = pair_source.shape[0]
    band = lats // devices
    turned = frames.transpose(0, 1, 3, 2).reshape(variables * lons, lats)

    def spread(rows):
        return lax.all_to_all(
            rows.reshape(devices, -1, rows.shape[1]), "space", split_axis=0, concat_axis=0, tiled=True
        ).reshape(rows.shape)

    strips = spread(pack_frames(turned))

    target = pair_device[:, 0]
    order = jnp.arange(count, dtype=jnp.int32)
    earlier = (target[:, None] == target[None, :]) & (order[:, None] < order[None, :])
    rank = jnp.sum(earlier.astype(jnp.int32), axis=0)
    place = target * 2 + rank
    columns = devices // 8
    first_row = (pair_source % columns) * 32 + pair_source // columns
    row = jnp.arange(devices * 8, dtype=jnp.int32)
    hit = (place[None, :] == (row >> 2)[:, None]).astype(jnp.int32)
    shift = 16384
    wanted = jnp.sum(hit * (first_row + shift)[None, :], axis=1) + (row & 3) * band
    block = jnp.sum(hit * (pair_local + 1)[None, :], axis=1)
    matrix = jnp.sum(hit * pair_matrix[None, :], axis=1)
    pick = (wanted[:, None] == (jnp.arange(lats // 2, dtype=jnp.int32) + shift)[None, :]).astype(
        jnp.bfloat16
    )
    lane = jnp.arange(LANES, dtype=jnp.int32)[None, :]
    meta = jnp.where(
        lane == META_BLOCK, block[:, None], jnp.where(lane == META_MATRIX, matrix[:, None], 0)
    ).astype(jnp.bfloat16)

    received = spread(select_rows(pick, meta, strips))

    kinds, _, cells = regrid_mats.shape
    split = regrid_mats.reshape(kinds, 2, 4, 8, cells).transpose(4, 3, 1, 0, 2)
    even = split.reshape(cells, -1)
    odd = split[:, :, ::-1].reshape(cells, -1)
    field = regrid(received, even, odd)
    padded_field = field.reshape(PAD_SIDE, PAD_SIDE, BLK_DEV, VPAD)[..., :variables]
    padded_field = padded_field.transpose(2, 0, 1, 3)
    first_out = conv_valid(padded_field, w_first, ("NHWC", "HWIO", "NHWC")) + b_first
    hidden = jax.nn.gelu(first_out, approximate=True).astype(jnp.bfloat16)
    second = conv_valid(hidden, w_second, ("NHWC", "HWIO", "NHWC")) + b_second
    return second.astype(jnp.bfloat16).reshape(1, BLK_DEV, SIDE * SIDE, -1)


def solution(mesh):
    in_specs = (
        P("tm", None, None, "space"),
        P(),
        P("space"),
        P("space"),
        P("space", None),
        P("space"),
        P(),
        P(),
        P(),
        P(),
    )
    out_specs = P("tm", "space", None, None)
    return jax.shard_map(
        per_device, mesh=mesh, in_specs=in_specs, out_specs=out_specs, check_vma=False
    )
```

```python
import jax
import jax.numpy as jnp
from jax import lax
from jax.experimental import pallas as pl
from jax.experimental.pallas import tpu as pltpu
from jax.sharding import PartitionSpec as P

SIDE = 8
BLK_DEV = 12
PAD_SIDE = 12
VPAD = 80
LANES = 128
META_BLOCK = 32
META_MATRIX = 33
VARIABLES = 73
WIDE = 19 * LANES
INTERPRET = False


def resident(array):
    return array if INTERPRET else pltpu.with_memory_space_constraint(array, pltpu.VMEM)


def resident_output(shape):
    struct = jax.ShapeDtypeStruct(shape, jnp.bfloat16)
    return struct if INTERPRET else pltpu.VMEM(shape, jnp.bfloat16)


IN_VMEM = pl.BlockSpec(memory_space=pltpu.VMEM)


def conv_valid(inputs, weights, layout):
    return lax.conv_general_dilated(
        inputs,
        weights,
        (1, 1),
        "VALID",
        dimension_numbers=layout,
        preferred_element_type=jnp.float32,
    )


def pack_kernel(x_ref, o_ref):
    depth = x_ref.shape[0]
    count, width = o_ref.shape
    o_ref[:, :depth] = x_ref[...].T
    o_ref[:, depth:] = jnp.zeros((count, width - depth), jnp.bfloat16)


def pack_frames(rows):
    depth, lats = rows.shape
    width = 8 * VPAD
    step = 256
    return pl.pallas_call(
        pack_kernel,
        grid=(lats // step,),
        in_specs=[pl.BlockSpec((depth, step), lambda i: (0, i))],
        out_specs=pl.BlockSpec((step, width), lambda i: (i, 0)),
        out_shape=jax.ShapeDtypeStruct((lats, width), jnp.bfloat16),
        interpret=INTERPRET,
    )(rows)


def select_kernel(pick_ref, meta_ref, x_ref, o_ref, wide_ref):
    depth = pick_ref.shape[1]
    width = wide_ref.shape[1]
    cells = 8 * VARIABLES
    tile = width - LANES

    @pl.when(pl.program_id(0) == 0)
    def _():
        wide_ref[:, tile:] = jnp.zeros((depth, LANES), jnp.bfloat16)
        for part in range(4):
            x = x_ref[:, part].reshape(depth, x_ref.shape[-1])
            wide_ref[:, part * cells : (part + 1) * cells] = x[:, :cells]

    out = jnp.dot(pick_ref[...], wide_ref[...], preferred_element_type=jnp.float32)
    meta = meta_ref[...].astype(jnp.float32)
    lead = o_ref.shape[:2]
    o_ref[:, :, :tile] = out[:, :tile].astype(jnp.bfloat16).reshape(*lead, tile)
    o_ref[:, :, tile:] = (out[:, tile:] + meta).astype(jnp.bfloat16).reshape(*lead, LANES)


def select_rows(pick, meta, strips):
    count, depth = pick.shape
    strips = strips.reshape(-1, 4, 16, strips.shape[-1])
    step = 256
    return pl.pallas_call(
        select_kernel,
        grid=(count // step,),
        in_specs=[
            pl.BlockSpec((step, depth), lambda i: (i, 0)),
            pl.BlockSpec((step, LANES), lambda i: (i, 0)),
            IN_VMEM,
        ],
        out_specs=pl.BlockSpec((step // 4, 4, WIDE), lambda i: (i, 0, 0)),
        out_shape=jax.ShapeDtypeStruct((count // 4, 4, WIDE), jnp.bfloat16),
        scratch_shapes=[pltpu.VMEM((depth, WIDE), jnp.bfloat16)],
        interpret=INTERPRET,
    )(pick, meta, resident(strips))


def regrid_kernel(r_ref, mats_ref, o_ref, sum_ref, turn_ref):
    groups = BLK_DEV // 4
    lanes = groups * LANES
    count = r_ref.shape[0] * r_ref.shape[1]
    width = r_ref.shape[2]
    cells = 8 * VARIABLES
    rows = r_ref[...].reshape(count, width)
    kind = lax.broadcasted_iota(jnp.int32, (LANES, lanes), 0)
    weight = jnp.where(kind == META_BLOCK, 32.0, jnp.where(kind == META_MATRIX, 2.0, 0.0))
    step = lax.broadcasted_iota(jnp.int32, (count, lanes), 0) & 1
    base = step.astype(jnp.float32) + jnp.dot(
        rows[:, width - LANES :], weight.astype(jnp.bfloat16), preferred_element_type=jnp.float32
    )
    lane = lax.broadcasted_iota(jnp.int32, (1, lanes), 1)
    turned = rows.T
    for part in range(4):
        code = base - ((lane ^ (32 * part)) + 32).astype(jnp.float32)
        mine = jnp.where(code == 0.0, 1.0, 0.0).astype(jnp.bfloat16)
        got = jnp.dot(
            turned[part * cells : (part + 1) * cells], mine, preferred_element_type=jnp.float32
        )
        for group in range(groups):
            first = (part * groups + group) * cells
            sum_ref[first : first + cells, :] = got[:, group * LANES : (group + 1) * LANES]
    variables = VARIABLES
    spot = lax.broadcasted_iota(jnp.int32, (variables, LANES), 1) >> 5
    even = (spot & 1) == 0
    low = spot < 2
    for group in range(groups):
        stacks = [[], [], [], []]
        for w in range(8):
            parts = [
                sum_ref[pl.ds((part * groups + group) * cells + w, variables, stride=8), :]
                for part in range(4)
            ]
            for turn in range(4):
                one, two, three, four = (parts[turn ^ p] for p in range(4))
                mixed = jnp.where(low, jnp.where(even, one, two), jnp.where(even, three, four))
                stacks[turn].append(mixed.astype(jnp.bfloat16))
        for turn in range(4):
            field = lax.dot_general(
                mats_ref[turn],
                jnp.concatenate(stacks[turn], axis=1),
                (((1,), (1,)), ((), ())),
                preferred_element_type=jnp.float32,
            )
            turn_ref[pl.ds(4 * group + turn, field.shape[0], stride=16), :variables] = field
    count = o_ref.shape[0]
    o_ref[...] = (
        turn_ref[...].reshape(count, 16, LANES)[:, :BLK_DEV, :variables].astype(jnp.bfloat16)
    )


def regrid(rows, mats, variables):
    cells = mats.shape[1]
    return pl.pallas_call(
        regrid_kernel,
        in_specs=[IN_VMEM, IN_VMEM],
        out_specs=IN_VMEM,
        out_shape=resident_output((cells, BLK_DEV, variables)),
        scratch_shapes=[
            pltpu.VMEM((BLK_DEV * variables * 8, LANES), jnp.float32),
            pltpu.VMEM((16 * cells, LANES), jnp.float32),
        ],
        interpret=INTERPRET,
    )(rows, resident(mats))


def per_device(
    frames,
    regrid_mats,
    pair_source,
    pair_matrix,
    pair_device,
    pair_local,
    w_first,
    b_first,
    w_second,
    b_second,
):
    devices = lax.axis_size("space")
    _, variables, lats, lons = frames.shape
    count = pair_source.shape[0]
    band = lats // devices
    turned = frames.transpose(0, 1, 3, 2).reshape(variables * lons, lats)

    def spread(rows):
        return lax.all_to_all(rows, "space", split_axis=0, concat_axis=0, tiled=True)

    strips = spread(pack_frames(turned).reshape(devices, band, -1))

    target = pair_device[:, 0]
    order = jnp.arange(count, dtype=jnp.int32)
    earlier = (target[:, None] == target[None, :]) & (order[:, None] < order[None, :])
    rank = jnp.sum(earlier.astype(jnp.int32), axis=0)
    place = target * 2 + rank
    columns = devices // 8
    first_row = (pair_source % columns) * 16 + pair_source // columns
    row = jnp.arange(devices * 4, dtype=jnp.int32)
    hit = (place[None, :] == (row >> 1)[:, None]).astype(jnp.int32)
    shift = 16384
    wanted = jnp.sum(hit * (first_row + shift)[None, :], axis=1) + (row & 1) * band
    block = jnp.sum(hit * (pair_local + 1)[None, :], axis=1)
    matrix = jnp.sum(hit * pair_matrix[None, :], axis=1)
    pick = (wanted[:, None] == (jnp.arange(lats // 4, dtype=jnp.int32) + shift)[None, :]).astype(
        jnp.bfloat16
    )
    lane = jnp.arange(LANES, dtype=jnp.int32)[None, :]
    meta = jnp.where(
        lane == META_BLOCK, block[:, None], jnp.where(lane == META_MATRIX, matrix[:, None], 0)
    ).astype(jnp.bfloat16)

    received = spread(select_rows(pick, meta, strips))

    kinds, _, cells = regrid_mats.shape
    split = regrid_mats.reshape(kinds, 4, 2, 8, cells).transpose(4, 3, 1, 0, 2)
    mats = jnp.stack(
        [jnp.concatenate(
                [split[:, :, (turn ^ p) : (turn ^ p) + 1] for p in range(4)], axis=2
            ).reshape(cells, -1) for turn in range(4)]
    )
    field = regrid(received, mats, variables)
    padded_field = field.reshape(PAD_SIDE, PAD_SIDE, BLK_DEV, variables).transpose(2, 0, 1, 3)
    first_out = conv_valid(padded_field, w_first, ("NHWC", "HWIO", "NHWC")) + b_first
    hidden = jax.nn.gelu(first_out, approximate=True).astype(jnp.bfloat16)
    second = conv_valid(hidden, w_second, ("NHWC", "HWIO", "NHWC")) + b_second
    return second.astype(jnp.bfloat16).reshape(1, BLK_DEV, SIDE * SIDE, -1)


def solution(mesh):
    in_specs = (
        P("tm", None, None, "space"),
        P(),
        P("space"),
        P("space"),
        P("space", None),
        P("space"),
        P(),
        P(),
        P(),
        P(),
    )
    out_specs = P("tm", "space", None, None)
    return jax.shard_map(
        per_device, mesh=mesh, in_specs=in_specs, out_specs=out_specs, check_vma=False
    )
```

```python
import jax
import jax.numpy as jnp
from jax import lax
from jax.experimental import pallas as pl
from jax.experimental.pallas import tpu as pltpu
from jax.sharding import PartitionSpec as P

SIDE = 8
BLK_DEV = 12
PAD_SIDE = 12
VPAD = 80
LANES = 128
META_BLOCK = 32
META_MATRIX = 33
VARIABLES = 73
WIDE = 19 * LANES
INTERPRET = False


def resident(array):
    return array if INTERPRET else pltpu.with_memory_space_constraint(array, pltpu.VMEM)


def resident_output(shape):
    struct = jax.ShapeDtypeStruct(shape, jnp.bfloat16)
    return struct if INTERPRET else pltpu.VMEM(shape, jnp.bfloat16)


IN_VMEM = pl.BlockSpec(memory_space=pltpu.VMEM)


def conv_valid(inputs, weights, layout):
    return lax.conv_general_dilated(
        inputs,
        weights,
        (1, 1),
        "VALID",
        dimension_numbers=layout,
        preferred_element_type=jnp.float32,
    )


def pack_kernel(x_ref, o_ref):
    depth = x_ref.shape[0]
    count, width = o_ref.shape
    o_ref[:, :depth] = x_ref[...].T
    o_ref[:, depth:] = jnp.zeros((count, width - depth), jnp.bfloat16)


def pack_frames(rows):
    depth, lats = rows.shape
    width = 8 * VPAD
    step = 512
    return pl.pallas_call(
        pack_kernel,
        grid=(lats // step,),
        in_specs=[pl.BlockSpec((depth, step), lambda i: (0, i))],
        out_specs=pl.BlockSpec((step, width), lambda i: (i, 0)),
        out_shape=jax.ShapeDtypeStruct((lats, width), jnp.bfloat16),
        interpret=INTERPRET,
    )(rows)


def select_kernel(pick_ref, meta_ref, x_ref, o_ref, wide_ref):
    depth = pick_ref.shape[1]
    width = wide_ref.shape[1]
    cells = 8 * VARIABLES
    tile = width - LANES

    @pl.when(pl.program_id(0) == 0)
    def _():
        wide_ref[:, tile:] = jnp.zeros((depth, LANES), jnp.bfloat16)
        for part in range(4):
            x = x_ref[:, part].reshape(depth, x_ref.shape[-1])
            wide_ref[:, part * cells : (part + 1) * cells] = x[:, :cells]

    out = jnp.dot(pick_ref[...], wide_ref[...], preferred_element_type=jnp.float32)
    meta = meta_ref[...].astype(jnp.float32)
    lead = o_ref.shape[:2]
    o_ref[:, :, :tile] = out[:, :tile].astype(jnp.bfloat16).reshape(*lead, tile)
    o_ref[:, :, tile:] = (out[:, tile:] + meta).astype(jnp.bfloat16).reshape(*lead, LANES)


def select_rows(pick, meta, strips):
    count, depth = pick.shape
    strips = strips.reshape(-1, 4, 16, strips.shape[-1])
    step = 256
    return pl.pallas_call(
        select_kernel,
        grid=(count // step,),
        in_specs=[
            pl.BlockSpec((step, depth), lambda i: (i, 0)),
            pl.BlockSpec((step, LANES), lambda i: (i, 0)),
            IN_VMEM,
        ],
        out_specs=pl.BlockSpec((step // 4, 4, WIDE), lambda i: (i, 0, 0)),
        out_shape=jax.ShapeDtypeStruct((count // 4, 4, WIDE), jnp.bfloat16),
        scratch_shapes=[pltpu.VMEM((depth, WIDE), jnp.bfloat16)],
        interpret=INTERPRET,
    )(pick, meta, resident(strips))


def regrid_kernel(r_ref, mats_ref, o_ref, sum_ref, turn_ref):
    groups = BLK_DEV // 4
    lanes = groups * LANES
    count = r_ref.shape[0] * r_ref.shape[1]
    width = r_ref.shape[2]
    cells = 8 * VARIABLES
    rows = r_ref[...].reshape(count, width)
    kind = lax.broadcasted_iota(jnp.int32, (LANES, lanes), 0)
    weight = jnp.where(kind == META_BLOCK, 32.0, jnp.where(kind == META_MATRIX, 2.0, 0.0))
    step = lax.broadcasted_iota(jnp.int32, (count, lanes), 0) & 1
    base = step.astype(jnp.float32) + jnp.dot(
        rows[:, width - LANES :], weight.astype(jnp.bfloat16), preferred_element_type=jnp.float32
    )
    lane = lax.broadcasted_iota(jnp.int32, (1, lanes), 1)
    turned = rows.T
    for part in range(4):
        code = base - ((lane ^ (32 * part)) + 32).astype(jnp.float32)
        mine = jnp.where(code == 0.0, 1.0, 0.0).astype(jnp.bfloat16)
        got = jnp.dot(
            turned[part * cells : (part + 1) * cells], mine, preferred_element_type=jnp.float32
        )
        for group in range(groups):
            first = (part * groups + group) * cells
            sum_ref[first : first + cells, :] = got[:, group * LANES : (group + 1) * LANES]
    sum_ref[4 * groups * cells :, :] = jnp.zeros((LANES, LANES), jnp.float32)
    spot = lax.broadcasted_iota(jnp.int32, (VPAD, LANES), 1) >> 5
    even = (spot & 1) == 0
    low = spot < 2
    stacks = [[], [], [], []]
    for group in range(groups):
        wide = [[], [], [], []]
        for w in range(8):
            parts = [
                sum_ref[pl.ds((part * groups + group) * cells + w, VPAD, stride=8), :]
                for part in range(4)
            ]
            for turn in range(4):
                one, two, three, four = (parts[turn ^ p] for p in range(4))
                mixed = jnp.where(low, jnp.where(even, one, two), jnp.where(even, three, four))
                wide[turn].append(mixed.astype(jnp.bfloat16))
        for turn in range(4):
            stacks[turn].append(jnp.concatenate(wide[turn], axis=1))
    for turn in range(4):
        fields = lax.dot_general(
            mats_ref[turn],
            jnp.concatenate(stacks[turn], axis=0),
            (((1,), (1,)), ((), ())),
            preferred_element_type=jnp.float32,
        )
        for group in range(groups):
            field = fields[:, group * VPAD : (group + 1) * VPAD]
            turn_ref[pl.ds(4 * group + turn, field.shape[0], stride=16), :VPAD] = field
    count = o_ref.shape[0]
    o_ref[...] = (
        turn_ref[...].reshape(count, 16, LANES)[:, :BLK_DEV, : o_ref.shape[2]].astype(jnp.bfloat16)
    )


def regrid(rows, mats, variables):
    cells = mats.shape[1]
    return pl.pallas_call(
        regrid_kernel,
        in_specs=[IN_VMEM, IN_VMEM],
        out_specs=IN_VMEM,
        out_shape=resident_output((cells, BLK_DEV, variables)),
        scratch_shapes=[
            pltpu.VMEM((BLK_DEV * variables * 8 + LANES, LANES), jnp.float32),
            pltpu.VMEM((16 * cells, LANES), jnp.float32),
        ],
        interpret=INTERPRET,
    )(rows, resident(mats))


def per_device(
    frames,
    regrid_mats,
    pair_source,
    pair_matrix,
    pair_device,
    pair_local,
    w_first,
    b_first,
    w_second,
    b_second,
):
    devices = lax.axis_size("space")
    _, variables, lats, lons = frames.shape
    count = pair_source.shape[0]
    band = lats // devices
    turned = frames.transpose(0, 1, 3, 2).reshape(variables * lons, lats)

    def spread(rows):
        return lax.all_to_all(rows, "space", split_axis=0, concat_axis=0, tiled=True)

    strips = spread(pack_frames(turned).reshape(devices, band, -1))

    target = pair_device[:, 0]
    order = jnp.arange(count, dtype=jnp.int32)
    earlier = (target[:, None] == target[None, :]) & (order[:, None] < order[None, :])
    rank = jnp.sum(earlier.astype(jnp.int32), axis=0)
    place = target * 2 + rank
    columns = devices // 8
    first_row = (pair_source % columns) * 16 + pair_source // columns
    row = jnp.arange(devices * 4, dtype=jnp.int32)
    hit = (place[None, :] == (row >> 1)[:, None]).astype(jnp.int32)
    shift = 16384
    wanted = jnp.sum(hit * (first_row + shift)[None, :], axis=1) + (row & 1) * band
    block = jnp.sum(hit * (pair_local + 1)[None, :], axis=1)
    matrix = jnp.sum(hit * pair_matrix[None, :], axis=1)
    pick = (wanted[:, None] == (jnp.arange(lats // 4, dtype=jnp.int32) + shift)[None, :]).astype(
        jnp.bfloat16
    )
    lane = jnp.arange(LANES, dtype=jnp.int32)[None, :]
    meta = jnp.where(
        lane == META_BLOCK, block[:, None], jnp.where(lane == META_MATRIX, matrix[:, None], 0)
    ).astype(jnp.bfloat16)

    received = spread(select_rows(pick, meta, strips))

    kinds, _, cells = regrid_mats.shape
    split = regrid_mats.reshape(kinds, 4, 2, 8, cells).transpose(4, 3, 1, 0, 2)
    mats = jnp.stack(
        [jnp.concatenate(
                [split[:, :, (turn ^ p) : (turn ^ p) + 1] for p in range(4)], axis=2
            ).reshape(cells, -1) for turn in range(4)]
    )
    field = regrid(received, mats, variables)
    padded_field = field.reshape(PAD_SIDE, PAD_SIDE, BLK_DEV, variables).transpose(2, 0, 1, 3)
    first_out = conv_valid(padded_field, w_first, ("NHWC", "HWIO", "NHWC")) + b_first
    hidden = jax.nn.gelu(first_out, approximate=True).astype(jnp.bfloat16)
    second = conv_valid(hidden, w_second, ("NHWC", "HWIO", "NHWC")) + b_second
    return second.astype(jnp.bfloat16).reshape(1, BLK_DEV, SIDE * SIDE, -1)


def solution(mesh):
    in_specs = (
        P("tm", None, None, "space"),
        P(),
        P("space"),
        P("space"),
        P("space", None),
        P("space"),
        P(),
        P(),
        P(),
        P(),
    )
    out_specs = P("tm", "space", None, None)
    return jax.shard_map(
        per_device, mesh=mesh, in_specs=in_specs, out_specs=out_specs, check_vma=False
    )
```

```python
import jax
import jax.numpy as jnp
from jax import lax
from jax.experimental import pallas as pl
from jax.experimental.pallas import tpu as pltpu
from jax.sharding import PartitionSpec as P

SIDE = 8
BLK_DEV = 12
PAD_SIDE = 12
VPAD = 80
LANES = 128
META = 64
VARIABLES = 73
WIDE = 37 * LANES
INTERPRET = False


def resident(array):
    return array if INTERPRET else pltpu.with_memory_space_constraint(array, pltpu.VMEM)


def resident_output(shape):
    struct = jax.ShapeDtypeStruct(shape, jnp.bfloat16)
    return struct if INTERPRET else pltpu.VMEM(shape, jnp.bfloat16)


IN_VMEM = pl.BlockSpec(memory_space=pltpu.VMEM)


def conv_valid(inputs, weights, layout):
    return lax.conv_general_dilated(
        inputs,
        weights,
        (1, 1),
        "VALID",
        dimension_numbers=layout,
        preferred_element_type=jnp.float32,
    )


def pack_kernel(x_ref, o_ref):
    depth = x_ref.shape[0]
    count, width = o_ref.shape
    o_ref[:, :depth] = x_ref[...].T
    o_ref[:, depth:] = jnp.zeros((count, width - depth), jnp.bfloat16)


def pack_frames(rows):
    depth, lats = rows.shape
    width = 8 * VPAD
    step = 512
    return pl.pallas_call(
        pack_kernel,
        grid=(lats // step,),
        in_specs=[pl.BlockSpec((depth, step), lambda i: (0, i))],
        out_specs=pl.BlockSpec((step, width), lambda i: (i, 0)),
        out_shape=jax.ShapeDtypeStruct((lats, width), jnp.bfloat16),
        interpret=INTERPRET,
    )(rows)


def select_kernel(one_ref, two_ref, meta_ref, x_ref, o_ref, near_ref, far_ref):
    depth, width = near_ref.shape
    cells = 8 * VARIABLES
    skip = 4 * cells % LANES
    tile = width - LANES

    @pl.when(pl.program_id(0) == 0)
    def _():
        near_ref[:, tile:] = jnp.zeros((depth, LANES), jnp.bfloat16)
        far_ref[:, :LANES] = jnp.zeros((depth, LANES), jnp.bfloat16)
        far_ref[:, tile:] = jnp.zeros((depth, LANES), jnp.bfloat16)
        for part in range(4):
            x = x_ref[:, part].reshape(depth, x_ref.shape[-1])[:, :cells]
            near_ref[:, part * cells : (part + 1) * cells] = x
            far_ref[:, skip + part * cells : skip + (part + 1) * cells] = x

    lead = o_ref.shape[:2]

    def put(first, value):
        size = value.shape[1]
        o_ref[:, :, first : first + size] = value.astype(jnp.bfloat16).reshape(*lead, size)

    near = jnp.dot(one_ref[...], near_ref[...], preferred_element_type=jnp.float32)
    far = jnp.dot(two_ref[...], far_ref[...], preferred_element_type=jnp.float32)
    put(0, near[:, :tile])
    put(tile, near[:, tile:] + far[:, :LANES])
    put(width, far[:, LANES:tile])
    put(tile + tile, far[:, tile:] + meta_ref[...].astype(jnp.float32))


def select_rows(pick, meta, strips):
    count, depth = meta.shape[0], pick.shape[1]
    strips = strips.reshape(-1, 4, 16, strips.shape[-1])
    step = 128
    half = WIDE // LANES // 2 * LANES + LANES
    return pl.pallas_call(
        select_kernel,
        grid=(count // step,),
        in_specs=[
            pl.BlockSpec((step, depth), lambda i: (i, 0)),
            pl.BlockSpec((step, depth), lambda i: (i + count // step, 0)),
            pl.BlockSpec((step, LANES), lambda i: (i, 0)),
            IN_VMEM,
        ],
        out_specs=pl.BlockSpec((step // 2, 2, WIDE), lambda i: (i, 0, 0)),
        out_shape=jax.ShapeDtypeStruct((count // 2, 2, WIDE), jnp.bfloat16),
        scratch_shapes=[pltpu.VMEM((depth, half), jnp.bfloat16) for _ in range(2)],
        interpret=INTERPRET,
    )(pick, pick, meta, resident(strips))


def regrid_kernel(r_ref, mats_ref, o_ref, sum_ref, turn_ref):
    groups = BLK_DEV // 4
    lanes = groups * LANES
    count = r_ref.shape[0] * r_ref.shape[1]
    width = r_ref.shape[2]
    cells = 8 * VARIABLES
    rows = r_ref[...].reshape(count, width)
    kind = lax.broadcasted_iota(jnp.int32, (LANES, lanes), 0)
    step = lax.broadcasted_iota(jnp.int32, (2 * count, lanes), 0) & 1
    found = []
    for slot in range(2):
        first = META + 2 * slot
        weight = jnp.where(kind == first, 32.0, jnp.where(kind == first + 1, 2.0, 0.0))
        found.append(
            jnp.dot(
                rows[:, width - LANES :],
                weight.astype(jnp.bfloat16),
                preferred_element_type=jnp.float32,
            )
        )
    base = jnp.concatenate(found, axis=0) + step.astype(jnp.float32)
    lane = lax.broadcasted_iota(jnp.int32, (1, lanes), 1)
    turned = rows.T
    for part in range(4):
        code = base - ((lane ^ (32 * part)) + 32).astype(jnp.float32)
        mine = jnp.where(code == 0.0, 1.0, 0.0).astype(jnp.bfloat16)
        both = jnp.concatenate(
            [turned[(4 * slot + part) * cells : (4 * slot + part + 1) * cells] for slot in range(2)],
            axis=1,
        )
        got = jnp.dot(both, mine, preferred_element_type=jnp.float32)
        for group in range(groups):
            first = (part * groups + group) * cells
            sum_ref[first : first + cells, :] = got[:, group * LANES : (group + 1) * LANES]
    sum_ref[4 * groups * cells :, :] = jnp.zeros((LANES, LANES), jnp.float32)
    spot = lax.broadcasted_iota(jnp.int32, (VPAD, LANES), 1) >> 5
    even = (spot & 1) == 0
    low = spot < 2
    stacks = [[], [], [], []]
    for group in range(groups):
        wide = [[], [], [], []]
        for w in range(8):
            parts = [
                sum_ref[pl.ds((part * groups + group) * cells + w, VPAD, stride=8), :]
                for part in range(4)
            ]
            for turn in range(4):
                one, two, three, four = (parts[turn ^ p] for p in range(4))
                mixed = jnp.where(low, jnp.where(even, one, two), jnp.where(even, three, four))
                wide[turn].append(mixed.astype(jnp.bfloat16))
        for turn in range(4):
            stacks[turn].append(jnp.concatenate(wide[turn], axis=1))
    for turn in range(4):
        fields = lax.dot_general(
            mats_ref[turn],
            jnp.concatenate(stacks[turn], axis=0),
            (((1,), (1,)), ((), ())),
            preferred_element_type=jnp.float32,
        )
        for group in range(groups):
            field = fields[:, group * VPAD : (group + 1) * VPAD]
            turn_ref[pl.ds(4 * group + turn, field.shape[0], stride=16), :VPAD] = field
    count = o_ref.shape[0]
    o_ref[...] = (
        turn_ref[...].reshape(count, 16, LANES)[:, :BLK_DEV, : o_ref.shape[2]].astype(jnp.bfloat16)
    )


def regrid(rows, mats, variables):
    cells = mats.shape[1]
    return pl.pallas_call(
        regrid_kernel,
        in_specs=[IN_VMEM, IN_VMEM],
        out_specs=IN_VMEM,
        out_shape=resident_output((cells, BLK_DEV, variables)),
        scratch_shapes=[
            pltpu.VMEM((BLK_DEV * variables * 8 + LANES, LANES), jnp.float32),
            pltpu.VMEM((16 * cells, LANES), jnp.float32),
        ],
        interpret=INTERPRET,
    )(rows, resident(mats))


def per_device(
    frames,
    regrid_mats,
    pair_source,
    pair_matrix,
    pair_device,
    pair_local,
    w_first,
    b_first,
    w_second,
    b_second,
):
    devices = lax.axis_size("space")
    _, variables, lats, lons = frames.shape
    count = pair_source.shape[0]
    band = lats // devices
    turned = frames.transpose(0, 1, 3, 2).reshape(variables * lons, lats)

    def spread(rows):
        return lax.all_to_all(rows, "space", split_axis=0, concat_axis=0, tiled=True)

    strips = spread(pack_frames(turned).reshape(devices, band, -1))

    target = pair_device[:, 0]
    order = jnp.arange(count, dtype=jnp.int32)
    earlier = (target[:, None] == target[None, :]) & (order[:, None] < order[None, :])
    rank = jnp.sum(earlier.astype(jnp.int32), axis=0)
    place = target * 2 + rank
    columns = devices // 8
    first_row = (pair_source % columns) * 16 + pair_source // columns
    row = jnp.arange(devices * 4, dtype=jnp.int32)
    slot = (row & (2 * devices - 1)) // 2 * 2 + row // (2 * devices)
    hit = (place[None, :] == slot[:, None]).astype(jnp.int32)
    shift = 16384
    wanted = jnp.sum(hit * (first_row + shift)[None, :], axis=1) + (row & 1) * band
    block = jnp.sum(hit * (pair_local + 1)[None, :], axis=1)
    matrix = jnp.sum(hit * pair_matrix[None, :], axis=1)
    pick = (wanted[:, None] == (jnp.arange(lats // 4, dtype=jnp.int32) + shift)[None, :]).astype(
        jnp.bfloat16
    )
    lane = jnp.arange(LANES, dtype=jnp.int32)[None, :]
    notes = jnp.stack([block, matrix]).reshape(2, 2, 2 * devices, 1)
    meta = jnp.where(
        lane == META,
        notes[0, 0],
        jnp.where(
            lane == META + 1,
            notes[1, 0],
            jnp.where(lane == META + 2, notes[0, 1], jnp.where(lane == META + 3, notes[1, 1], 0)),
        ),
    ).astype(jnp.bfloat16)

    received = spread(select_rows(pick, meta, strips))

    kinds, _, cells = regrid_mats.shape
    split = regrid_mats.reshape(kinds, 4, 2, 8, cells).transpose(4, 3, 1, 0, 2)
    mats = jnp.stack(
        [jnp.concatenate(
                [split[:, :, (turn ^ p) : (turn ^ p) + 1] for p in range(4)], axis=2
            ).reshape(cells, -1) for turn in range(4)]
    )
    field = regrid(received, mats, variables)
    padded_field = field.reshape(PAD_SIDE, PAD_SIDE, BLK_DEV, variables).transpose(2, 0, 1, 3)
    first_out = conv_valid(padded_field, w_first, ("NHWC", "HWIO", "NHWC")) + b_first
    hidden = jax.nn.gelu(first_out, approximate=True).astype(jnp.bfloat16)
    second = conv_valid(hidden, w_second, ("NHWC", "HWIO", "NHWC")) + b_second
    return second.astype(jnp.bfloat16).reshape(1, BLK_DEV, SIDE * SIDE, -1)


def solution(mesh):
    in_specs = (
        P("tm", None, None, "space"),
        P(),
        P("space"),
        P("space"),
        P("space", None),
        P("space"),
        P(),
        P(),
        P(),
        P(),
    )
    out_specs = P("tm", "space", None, None)
    return jax.shard_map(
        per_device, mesh=mesh, in_specs=in_specs, out_specs=out_specs, check_vma=False
    )
```
